32 devices in a mesh: ens: 2 (over y), grid: 4 (over z), pole: 4 (over x, core).
Axes of the slice: x: 2, y: 2, z: 4, core: 2. Of those that a mesh axis runs over, the one named last changes fastest.
Arguments:
- inverse_pool: bfloat16 [8, 2, 4096, 4096], P(('ens', 'pole'), None, 'grid'), parts along dimension 0, may hold values from -6 to 6
- factor_tiles: bfloat16 [8, 4, 2, 10, 256, 256], P(('ens', 'pole'), None, None, None, 'grid'), parts along dimension 0, may hold values from -0.078125 to 0.078125
- diag_inverse: bfloat16 [8, 2, 1024, 256], P(('ens', 'pole'), None, 'grid'), parts along dimension 0, may hold values from -6 to 6
- pole_weight: float32 [4, 2], P('pole'), may hold values from -3 to 3
- ancestors: int32 [4, 10], replicated, may hold values from 0 to 15, all different within a row
Outputs:
- density_panel: float32 [8192, 1024], P(('ens', 'grid'), 'pole'), parts along dimension 0
- density_diagonal: float32 [2048, 256], P(('ens', 'grid')), parts along dimension 0
The draws below stay inside these ranges and needn't reach their ends.
There are 2 independent parts, one for each index of `ens`. The reference program is written for one: setup_inputs(seed, part) draws one part's arguments, and reference() takes and returns one part's arrays. A program takes and returns all parts, laid end to end along the dimension named above; an argument that names none is the same for every part. Nothing has to cross between parts.
Inputs may be any that keep to these rules, and one draw needn't show every extreme that they name: `ancestors`: each row names 10 different ancestor blocks; every one of the 16 blocks is named by some row.
All inputs are finite; a program needn't handle non-finite values.
Results may differ from the reference program's by a relative error of at most 0.0022.
Values may be sent and summed in bfloat16 or wider, within the bound.
A program may use at most 128 MiB of HBM per device.

```python
import jax
import jax.numpy as jnp
from jax import lax

W = 256
NA = 16
ANC = 10
SUPER = 4
POLES = 4


def block_scale(rng, shape, split, least, largest):
    gain = 1.0
    for position, parts in split:
        steps = jax.random.uniform(jax.random.fold_in(jax.random.fold_in(rng, 6), position), (parts,), jnp.float32, least / len(split), largest / len(split))
        gain = gain * jnp.repeat(jnp.exp(steps), shape[position] // parts).reshape((-1,) + (1,) * (len(shape) - 1 - position))
    return gain


def different_ones(stream_key, rows, amount, top, lift):
    sequence = jax.random.permutation(jax.random.fold_in(stream_key, 1), amount)
    boost = sequence
    for power in range(3):
        boost = boost * boost // amount
    boost = boost * lift // amount
    tickets = jax.random.randint(jax.random.fold_in(stream_key, 2), (rows, amount), 0, 4096) + boost
    sure = jax.random.permutation(jax.random.fold_in(stream_key, 3), rows)[jnp.arange(amount) % rows]
    tickets = jnp.where(jnp.arange(rows)[:, None] == sure[None, :], 1 << 14, tickets)
    priority = tickets * amount + jnp.arange(amount)
    return lax.top_k(priority.astype(jnp.int32), top)[1].astype(jnp.int32)


def scatter_about(rng, shape, deviation, bound, split=(), kind=jnp.bfloat16):
    entries = deviation * jax.random.normal(rng, shape, jnp.float32)
    if split:
        entries = entries * block_scale(rng, shape, split, -0.22, 0.18)
    return jnp.clip(entries, -bound, bound).astype(kind)


def setup_inputs(seed: int = 0, part: int = 0) -> dict:
    seeds = jax.random.split(jax.random.key(seed), 6)
    part_splits = jax.random.split(jax.random.fold_in(seeds[5], part), 6)
    inverse_pool = scatter_about(part_splits[0], (POLES, 2, NA * W, NA * W), 1.0, 6.0, ((0, 4), (2, 4)))
    factor_tiles = scatter_about(part_splits[1], (POLES, SUPER, 2, ANC, W, W), (2 * ANC * W) ** -0.5, 0.078125, ((0, 4), (4, 4)))
    diag_inverse = scatter_about(part_splits[2], (POLES, 2, SUPER * W, W), 1.0, 6.0, ((0, 4), (2, 4)))
    pole_weight = scatter_about(seeds[3], (POLES, 2), POLES ** -0.5, 3.0, ((0, 4),), jnp.float32)
    ancestors = different_ones(seeds[4], SUPER, NA, ANC, 10240)
    return dict(inverse_pool=inverse_pool, factor_tiles=factor_tiles, diag_inverse=diag_inverse, pole_weight=pole_weight, ancestors=ancestors)


def product(left, right):
    return jnp.dot(left, right, precision=lax.Precision.HIGHEST)


def reference(inverse_pool, factor_tiles, diag_inverse, pole_weight, ancestors):
    panel = jnp.zeros((NA * W, SUPER * W), jnp.float32)
    diagonal = jnp.zeros((SUPER * W, W), jnp.float32)
    offsets = jnp.arange(W, dtype=jnp.int32)
    columns_all = (ancestors[:, :, None].astype(jnp.int32) * W + offsets[None, None, :]).reshape(SUPER, ANC * W).astype(jnp.int32)
    for pole_index in range(POLES):
        weight_real = pole_weight[pole_index, 0]
        weight_imag = pole_weight[pole_index, 1]
        for supernode in range(SUPER):
            columns = columns_all[supernode]
            selected = inverse_pool[pole_index][:, columns][:, :, columns].astype(jnp.float32)
            stacked = factor_tiles[pole_index, supernode].astype(jnp.float32).reshape(2, ANC * W, W)
            column_real = -(product(selected[0], stacked[0]) - product(selected[1], stacked[1]))
            column_imag = -(product(selected[0], stacked[1]) + product(selected[1], stacked[0]))
            lower = supernode * W
            panel = panel.at[columns, lower:lower + W].add(weight_real * column_imag + weight_imag * column_real)
            rounded_real = lax.optimization_barrier(column_real.astype(jnp.bfloat16)).astype(jnp.float32)
            rounded_imag = lax.optimization_barrier(column_imag.astype(jnp.bfloat16)).astype(jnp.float32)
            block_tile = diag_inverse[pole_index, :, lower:lower + W].astype(jnp.float32)
            block_real = block_tile[0] - (product(stacked[0].T, rounded_real) - product(stacked[1].T, rounded_imag))
            block_imag = block_tile[1] - (product(stacked[0].T, rounded_imag) + product(stacked[1].T, rounded_real))
            diagonal = diagonal.at[lower:lower + W].add(weight_real * block_imag + weight_imag * block_real)
    return panel, diagonal
```

```python
import functools

import jax
import jax.numpy as jnp
from jax import lax
from jax.experimental import pallas as pl
from jax.experimental.pallas import tpu as pltpu
from jax.sharding import PartitionSpec as P

MESH = pl.DeviceIdType.MESH
HALVES = 2


def plain_product(left, right):
    return jnp.dot(left, right, preferred_element_type=jnp.float32)


def turned_product(left, right):
    return lax.dot_general(
        left, right, (((0,), (0,)), ((), ())), preferred_element_type=jnp.float32
    )


def portion_terms(rows_pair, block_index, offset, listed, factors, weights):
    tile_width = factors.shape[3]
    listed_count = factors.shape[1]
    height = rows_pair.shape[1]
    blocks = rows_pair.shape[2] // tile_width
    matches = listed == block_index

    def compute():
        chosen = rows_pair.reshape(2, height, blocks, tile_width)[:, :, listed, :].reshape(
            2, height, listed_count * tile_width
        )
        stacked = factors.reshape(2, listed_count * tile_width, tile_width)
        part_real = -(plain_product(chosen[0], stacked[0]) - plain_product(chosen[1], stacked[1]))
        part_imag = -(plain_product(chosen[0], stacked[1]) + plain_product(chosen[1], stacked[0]))
        panel_piece = weights[0] * part_imag + weights[1] * part_real
        rounded_real = part_real.astype(jnp.bfloat16)
        rounded_imag = part_imag.astype(jnp.bfloat16)
        position = jnp.sum(jnp.where(matches, jnp.arange(listed_count, dtype=jnp.int32), 0))
        matched = lax.dynamic_slice(
            factors, (jnp.int32(0), position, offset, jnp.int32(0)), (2, 1, height, tile_width)
        )[:, 0]
        diag_real = -(
            turned_product(matched[0], rounded_real) - turned_product(matched[1], rounded_imag)
        )
        diag_imag = -(
            turned_product(matched[0], rounded_imag) + turned_product(matched[1], rounded_real)
        )
        return (panel_piece, weights[0] * diag_imag + weights[1] * diag_real)

    def skipped():
        return (
            jnp.zeros((height, tile_width), jnp.float32),
            jnp.zeros((tile_width, tile_width), jnp.float32),
        )

    return lax.cond(jnp.any(matches), compute, skipped)


def rows_terms(rows_pair, row_first, listed, factors, weights):
    tile_width = factors.shape[3]
    height = rows_pair.shape[1]
    piece_rows = min(height, tile_width)
    panels = []
    diag_total = jnp.zeros((tile_width, tile_width), jnp.float32)
    for portion in range(height // piece_rows):
        row_start = row_first + portion * piece_rows
        panel_piece, diag_piece = portion_terms(
            rows_pair[:, portion * piece_rows : (portion + 1) * piece_rows],
            row_start // tile_width,
            row_start % tile_width,
            listed,
            factors,
            weights,
        )
        panels.append(panel_piece)
        diag_total = diag_total + diag_piece
    return (jnp.concatenate(panels, axis=0), diag_total)


def shards(inverse_pool, factor_tiles, diag_inverse, pole_weight, ancestors):
    device_index = lax.axis_index("grid")
    rows_here = inverse_pool.shape[2]
    supers = factor_tiles.shape[1]
    tile_width = factor_tiles.shape[5]
    row_slab = inverse_pool[0]
    weights = (pole_weight[0, 0], pole_weight[0, 1])
    row_first = device_index * rows_here
    own_panels = []
    diag_terms = []
    for supernode in range(supers):
        factors = lax.all_gather(factor_tiles[0, supernode], "grid", axis=2, tiled=True)
        listed = ancestors[supernode]
        own_panel, own_diag = rows_terms(row_slab, row_first, listed, factors, weights)
        diag_terms.append(own_diag)
        own_panels.append(own_panel)
    panel_rows = jnp.concatenate(own_panels, axis=1)
    panel_share = lax.psum_scatter(panel_rows, "pole", scatter_dimension=1, tiled=True)
    diag_term = jnp.stack(diag_terms, axis=0).reshape(supers * tile_width, tile_width)
    diag_local = diag_inverse[0]
    local_block = weights[0] * diag_local[1].astype(jnp.float32) + weights[1] * diag_local[
        0
    ].astype(jnp.float32)
    share_rows = local_block.shape[0]
    placed = lax.dynamic_update_slice(
        jnp.zeros_like(diag_term), local_block, (device_index * share_rows, jnp.int32(0))
    )
    spread = lax.psum_scatter(diag_term + placed, ("grid", "pole"), scatter_dimension=0, tiled=True)
    diag_share = lax.all_gather(spread, "pole", axis=0, tiled=True)
    return (panel_share, diag_share)


def fused_kernel(
    grid_size, pole_size, ancestors, weight, pool, tiles, diag_in,
    panel_out, diag_out,
    rows, sent_panel, got_panel, column, own_diag, diag_local, pole_sums, grid_send, grid_sums, final,
    pool_sem, tile_sem, diag_sem, up_sem, down_sem, arrive_sem,
    panel_send, panel_recv, a_send, a_recv, b_send, b_recv, c_send, c_recv, *factors,
):
    g = lax.axis_index("grid")
    q = lax.axis_index("pole")
    supers, listed_count = ancestors.shape
    half = factors[0].shape[3] // 2
    width = factors[0].shape[2]
    slice_rows = width // grid_size
    share = width // pole_size
    blocks = rows.shape[2] // width
    chunks = [(k, c) for k in range(supers) for c in range(HALVES)]

    tile_copies = []
    for j, (k, c) in enumerate(chunks):
        for part in range(2):
            copy = pltpu.make_async_copy(
                tiles.at[0, k, part, :, :, pl.ds(c * half, half)],
                factors[k].at[c, :, pl.ds(g * slice_rows, slice_rows), pl.ds(part * half, half)],
                tile_sem.at[j, part],
            )
            copy.start()
            tile_copies.append(copy)
    pool_copies = []
    for part in range(2):
        for a in range(rows.shape[1]):
            copy = pltpu.make_async_copy(
                pool.at[0, part, :, pl.ds(a * width, width)], rows.at[part, a], pool_sem.at[part, a]
            )
            copy.start()
            pool_copies.append(copy)
    diag_copy = pltpu.make_async_copy(diag_in.at[0], diag_local, diag_sem)
    diag_copy.start()

    barrier = pltpu.get_barrier_semaphore()
    for step in range(1, grid_size):
        pl.semaphore_signal(
            barrier, inc=1, device_id={"grid": lax.rem(g + step, grid_size)}, device_id_type=MESH
        )
    for step in range(1, pole_size):
        pl.semaphore_signal(
            barrier, inc=1, device_id={"pole": lax.rem(q + step, pole_size)}, device_id_type=MESH
        )
    pl.semaphore_wait(barrier, grid_size - 1 + pole_size - 1)

    def piece(j, source):
        k, c = chunks[j]
        return factors[k].at[c, :, pl.ds(source * slice_rows, slice_rows), :]

    def hop(j, source, up):
        return pltpu.make_async_remote_copy(
            src_ref=piece(j, source),
            dst_ref=piece(j, source),
            send_sem=(up_sem if up else down_sem).at[j, source],
            recv_sem=arrive_sem.at[j, source],
            device_id={"grid": g + 1 if up else g - 1},
            device_id_type=MESH,
        )

    def pass_on(j, distance):
        low = g - distance
        high = g + distance
        if distance:
            @pl.when(low >= 0)
            def _():
                hop(j, low, True).wait_recv()

        @pl.when(jnp.logical_and(low >= 0, g + 1 < grid_size))
        def _():
            hop(j, low, True).start()

        if distance:
            @pl.when(high < grid_size)
            def _():
                hop(j, high, False).wait_recv()

        @pl.when(jnp.logical_and(high < grid_size, g >= 1))
        def _():
            hop(j, high, False).start()

    for j in range(len(chunks)):
        tile_copies[2 * j].wait()
        tile_copies[2 * j + 1].wait()
        pass_on(j, 0)
    for copy in pool_copies:
        copy.wait()
    diag_copy.wait()
    for distance in range(1, grid_size - 1):
        for j in range(len(chunks)):
            pass_on(j, distance)

    w_real = weight[0, 0]
    w_imag = weight[0, 1]

    def panel_copy(j, k, c, slot):
        return pltpu.make_async_remote_copy(
            src_ref=sent_panel.at[k, c],
            dst_ref=got_panel.at[slot, c],
            send_sem=panel_send.at[j],
            recv_sem=panel_recv.at[slot, c],
            device_id={"pole": k},
            device_id_type=MESH,
        )

    def share_copy(k, r):
        return pltpu.make_async_remote_copy(
            src_ref=own_diag.at[k, pl.ds(r * share, share)],
            dst_ref=pole_sums.at[k, q],
            send_sem=a_send.at[k, r],
            recv_sem=a_recv.at[k, q],
            device_id={"pole": r},
            device_id_type=MESH,
        )

    def place_of(k, block):
        count = jnp.int32(0)
        position = jnp.int32(0)
        for n in range(listed_count):
            hit = (ancestors[k, n] == block).astype(jnp.int32)
            count = count + hit
            position = position + hit * n
        return count, jnp.clip(position, 0, listed_count - 1)

    for j, (k, c) in enumerate(chunks):
        pass_on(j, grid_size - 1)

        @pl.loop(0, blocks)
        def _(b):
            span = pl.ds(pl.multiple_of(b * width, width), width)
            with_real = jnp.zeros((width, 2 * half), jnp.float32)
            with_imag = jnp.zeros((width, 2 * half), jnp.float32)
            for n in range(listed_count):
                source = jnp.clip(ancestors[k, n], 0, rows.shape[1] - 1)
                factor = factors[k][c, n]
                with_real += jnp.dot(
                    rows[0, source, span, :], factor, preferred_element_type=jnp.float32
                )
                with_imag += jnp.dot(
                    rows[1, source, span, :], factor, preferred_element_type=jnp.float32
                )
            count, _ = place_of(k, g * blocks + b)
            keep = jnp.full((width, half), count, jnp.int32) > 0
            real = jnp.where(keep, with_imag[:, half:] - with_real[:, :half], 0.0)
            imag = jnp.where(keep, -(with_real[:, half:] + with_imag[:, :half]), 0.0)
            column[span, pl.ds(c * 2 * half, half)] = real.astype(jnp.bfloat16)
            column[span, pl.ds(c * 2 * half + half, half)] = imag.astype(jnp.bfloat16)
            term = w_real * imag + w_imag * real
            sent_panel[k, c, span, :] = term.astype(jnp.bfloat16)

            @pl.when(q == k)
            def _():
                panel_out[span, pl.ds(c * half, half)] = term

        @pl.when(q != k)
        def _():
            panel_copy(j, k, c, lax.rem(q - k + pole_size, pole_size) - 1).start()

        if c == HALVES - 1:
            for left in range(HALVES):
                for right in range(HALVES):
                    def add(b, total):
                        _, position = place_of(k, g * blocks + b)
                        span = pl.ds(pl.multiple_of(b * width, width), width)
                        return total + lax.dot_general(
                            factors[k][left, position],
                            column[span, pl.ds(right * 2 * half, 2 * half)],
                            (((0,), (0,)), ((), ())),
                            preferred_element_type=jnp.float32,
                        )

                    total = jnp.zeros((2 * half, 2 * half), jnp.float32)
                    for b in range(blocks):
                        total = add(b, total)
                    real = total[half:, half:] - total[:half, :half]
                    imag = -(total[:half, half:] + total[half:, :half])
                    own_diag[k, pl.ds(left * half, half), pl.ds(right * half, half)] = (
                        w_real * imag + w_imag * real
                    )

            @pl.when(g == k)
            def _():
                own_diag[k] = (
                    own_diag[k]
                    + w_real * diag_local[1].astype(jnp.float32)
                    + w_imag * diag_local[0].astype(jnp.float32)
                )

            pole_sums[k, q] = own_diag[k, pl.ds(pl.multiple_of(q * share, share), share), :]
            for r in range(pole_size):
                @pl.when(q != r)
                def _():
                    share_copy(k, r).start()

    def grid_copy(k):
        return pltpu.make_async_remote_copy(
            src_ref=grid_send.at[k],
            dst_ref=grid_sums.at[g],
            send_sem=b_send.at[k],
            recv_sem=b_recv.at[g],
            device_id={"grid": k},
            device_id_type=MESH,
        )

    def final_copy(r):
        mine = pl.ds(pl.multiple_of(q * share, share), share)
        return pltpu.make_async_remote_copy(
            src_ref=final.at[mine],
            dst_ref=final.at[mine],
            send_sem=c_send.at[r],
            recv_sem=c_recv.at[q],
            device_id={"pole": r},
            device_id_type=MESH,
        )

    def landing(buffer, semaphore):
        return pltpu.make_async_remote_copy(
            src_ref=buffer, dst_ref=buffer, send_sem=semaphore, recv_sem=semaphore,
            device_id={"pole": q}, device_id_type=MESH,
        )

    for k in range(supers):
        for r in range(pole_size):
            @pl.when(q != r)
            def _():
                landing(pole_sums.at[k, r], a_recv.at[k, r]).wait_recv()
        summed = pole_sums[k, 0]
        for r in range(1, pole_size):
            summed = summed + pole_sums[k, r]
        grid_send[k] = summed

        @pl.when(g != k)
        def _():
            grid_copy(k).start()

        @pl.when(g == k)
        def _():
            grid_sums[g] = grid_send[k]

    for s in range(grid_size):
        @pl.when(g != s)
        def _():
            landing(grid_sums.at[s], b_recv.at[s]).wait_recv()
    summed = grid_sums[0]
    for s in range(1, grid_size):
        summed = summed + grid_sums[s]
    final[pl.ds(pl.multiple_of(q * share, share), share), :] = summed
    for r in range(pole_size):
        @pl.when(q != r)
        def _():
            final_copy(r).start()

    for c in range(HALVES):
        for slot in range(pole_size - 1):
            landing(got_panel.at[slot, c], panel_recv.at[slot, c]).wait_recv()

        @pl.loop(0, blocks)
        def _(b):
            span = pl.ds(pl.multiple_of(b * width, width), width)
            lanes = pl.ds(c * half, half)
            total = panel_out[span, lanes]
            for slot in range(pole_size - 1):
                total = total + got_panel[slot, c, span, :].astype(jnp.float32)
            panel_out[span, lanes] = total

    for r in range(pole_size):
        @pl.when(q != r)
        def _():
            landing(final.at[pl.ds(r * share, share)], c_recv.at[r]).wait_recv()
    diag_out[...] = final[...]

    for distance in range(grid_size - 1):
        for j in range(len(chunks)):
            @pl.when(jnp.logical_and(g - distance >= 0, g + 1 < grid_size))
            def _():
                hop(j, g - distance, True).wait_send()

            @pl.when(jnp.logical_and(g + distance < grid_size, g >= 1))
            def _():
                hop(j, g + distance, False).wait_send()
    for j, (k, c) in enumerate(chunks):
        @pl.when(q != k)
        def _():
            panel_copy(j, k, c, lax.rem(q - k + pole_size, pole_size) - 1).wait_send()
    for k in range(supers):
        for r in range(pole_size):
            @pl.when(q != r)
            def _():
                share_copy(k, r).wait_send()

        @pl.when(g != k)
        def _():
            grid_copy(k).wait_send()
    for r in range(pole_size):
        @pl.when(q != r)
        def _():
            final_copy(r).wait_send()


def fused(grid_size, pole_size, inverse_pool, factor_tiles, diag_inverse, pole_weight, ancestors):
    supers, listed_count = ancestors.shape
    width = factor_tiles.shape[5]
    height = inverse_pool.shape[2]
    half = width // HALVES
    share = width // pole_size
    chunks = supers * HALVES
    dma = pltpu.SemaphoreType.DMA
    f32 = jnp.float32
    bf16 = jnp.bfloat16
    scratch = [
        pltpu.VMEM((2, inverse_pool.shape[3] // width, height, width), bf16),
        pltpu.VMEM((supers, HALVES, height, half), bf16),
        pltpu.VMEM((pole_size - 1, HALVES, height, half), bf16),
        pltpu.VMEM((height, 2 * width), bf16),
        pltpu.VMEM((supers, width, width), f32),
        pltpu.VMEM(diag_inverse.shape[1:], bf16),
        pltpu.VMEM((supers, pole_size, share, width), f32),
        pltpu.VMEM((supers, share, width), f32),
        pltpu.VMEM((grid_size, share, width), f32),
        pltpu.VMEM((width, width), f32),
        dma((2, inverse_pool.shape[3] // width)), dma((chunks, 2)), dma(()),
        dma((chunks, grid_size)), dma((chunks, grid_size)), dma((chunks, grid_size)),
        dma((chunks,)), dma((pole_size - 1, HALVES)),
        dma((supers, pole_size)), dma((supers, pole_size)),
        dma((supers,)), dma((grid_size,)),
        dma((pole_size,)), dma((pole_size,)),
    ] + [pltpu.VMEM((HALVES, listed_count, width, 2 * half), bf16)] * supers
    smem = pl.BlockSpec(memory_space=pltpu.SMEM)
    vmem = pl.BlockSpec(memory_space=pltpu.VMEM)
    anywhere = pl.BlockSpec(memory_space=pl.ANY)
    return pl.pallas_call(
        functools.partial(fused_kernel, grid_size, pole_size),
        out_shape=(
            jax.ShapeDtypeStruct((height, width), f32),
            jax.ShapeDtypeStruct((width, width), f32),
        ),
        in_specs=[smem, smem, anywhere, anywhere, anywhere],
        out_specs=(vmem, vmem),
        scratch_shapes=scratch,
        compiler_params=pltpu.CompilerParams(
            collective_id=0, has_side_effects=True, vmem_limit_bytes=56 * 2**20
        ),
    )(ancestors, pole_weight, inverse_pool, factor_tiles, diag_inverse)


def choose(grid_size, pole_size, inverse_pool, factor_tiles, diag_inverse, pole_weight, ancestors):
    supers = ancestors.shape[0]
    width = factor_tiles.shape[5]
    whole_blocks = inverse_pool.shape[2] % width == 0 and factor_tiles.shape[4] % 16 == 0
    if whole_blocks and supers == grid_size == pole_size and width % (HALVES * 128) == 0:
        return fused(
            grid_size, pole_size, inverse_pool, factor_tiles, diag_inverse, pole_weight, ancestors
        )
    return shards(inverse_pool, factor_tiles, diag_inverse, pole_weight, ancestors)


def solution(mesh):
    in_specs = (
        P(("ens", "pole"), None, "grid", None),
        P(("ens", "pole"), None, None, None, "grid", None),
        P(("ens", "pole"), None, "grid", None),
        P("pole", None),
        P(),
    )
    out_specs = (P(("ens", "grid"), "pole"), P(("ens", "grid"), None))
    body = functools.partial(choose, mesh.shape["grid"], mesh.shape["pole"])
    return jax.shard_map(body, mesh=mesh, in_specs=in_specs, out_specs=out_specs, check_vma=False)
```

```python
import functools

import jax
import jax.numpy as jnp
from jax import lax
from jax.experimental import pallas as pl
from jax.experimental.pallas import tpu as pltpu
from jax.sharding import PartitionSpec as P

MESH = pl.DeviceIdType.MESH
HALVES = 2


def plain_product(left, right):
    return jnp.dot(left, right, preferred_element_type=jnp.float32)


def turned_product(left, right):
    return lax.dot_general(
        left, right, (((0,), (0,)), ((), ())), preferred_element_type=jnp.float32
    )


def portion_terms(rows_pair, block_index, offset, listed, factors, weights):
    tile_width = factors.shape[3]
    listed_count = factors.shape[1]
    height = rows_pair.shape[1]
    blocks = rows_pair.shape[2] // tile_width
    matches = listed == block_index

    def compute():
        chosen = rows_pair.reshape(2, height, blocks, tile_width)[:, :, listed, :].reshape(
            2, height, listed_count * tile_width
        )
        stacked = factors.reshape(2, listed_count * tile_width, tile_width)
        part_real = -(plain_product(chosen[0], stacked[0]) - plain_product(chosen[1], stacked[1]))
        part_imag = -(plain_product(chosen[0], stacked[1]) + plain_product(chosen[1], stacked[0]))
        panel_piece = weights[0] * part_imag + weights[1] * part_real
        rounded_real = part_real.astype(jnp.bfloat16)
        rounded_imag = part_imag.astype(jnp.bfloat16)
        position = jnp.sum(jnp.where(matches, jnp.arange(listed_count, dtype=jnp.int32), 0))
        matched = lax.dynamic_slice(
            factors, (jnp.int32(0), position, offset, jnp.int32(0)), (2, 1, height, tile_width)
        )[:, 0]
        diag_real = -(
            turned_product(matched[0], rounded_real) - turned_product(matched[1], rounded_imag)
        )
        diag_imag = -(
            turned_product(matched[0], rounded_imag) + turned_product(matched[1], rounded_real)
        )
        return (panel_piece, weights[0] * diag_imag + weights[1] * diag_real)

    def skipped():
        return (
            jnp.zeros((height, tile_width), jnp.float32),
            jnp.zeros((tile_width, tile_width), jnp.float32),
        )

    return lax.cond(jnp.any(matches), compute, skipped)


def rows_terms(rows_pair, row_first, listed, factors, weights):
    tile_width = factors.shape[3]
    height = rows_pair.shape[1]
    piece_rows = min(height, tile_width)
    panels = []
    diag_total = jnp.zeros((tile_width, tile_width), jnp.float32)
    for portion in range(height // piece_rows):
        row_start = row_first + portion * piece_rows
        panel_piece, diag_piece = portion_terms(
            rows_pair[:, portion * piece_rows : (portion + 1) * piece_rows],
            row_start // tile_width,
            row_start % tile_width,
            listed,
            factors,
            weights,
        )
        panels.append(panel_piece)
        diag_total = diag_total + diag_piece
    return (jnp.concatenate(panels, axis=0), diag_total)


def shards(inverse_pool, factor_tiles, diag_inverse, pole_weight, ancestors):
    device_index = lax.axis_index("grid")
    rows_here = inverse_pool.shape[2]
    supers = factor_tiles.shape[1]
    tile_width = factor_tiles.shape[5]
    row_slab = inverse_pool[0]
    weights = (pole_weight[0, 0], pole_weight[0, 1])
    row_first = device_index * rows_here
    own_panels = []
    diag_terms = []
    for supernode in range(supers):
        factors = lax.all_gather(factor_tiles[0, supernode], "grid", axis=2, tiled=True)
        listed = ancestors[supernode]
        own_panel, own_diag = rows_terms(row_slab, row_first, listed, factors, weights)
        diag_terms.append(own_diag)
        own_panels.append(own_panel)
    panel_rows = jnp.concatenate(own_panels, axis=1)
    panel_share = lax.psum_scatter(panel_rows, "pole", scatter_dimension=1, tiled=True)
    diag_term = jnp.stack(diag_terms, axis=0).reshape(supers * tile_width, tile_width)
    diag_local = diag_inverse[0]
    local_block = weights[0] * diag_local[1].astype(jnp.float32) + weights[1] * diag_local[
        0
    ].astype(jnp.float32)
    share_rows = local_block.shape[0]
    placed = lax.dynamic_update_slice(
        jnp.zeros_like(diag_term), local_block, (device_index * share_rows, jnp.int32(0))
    )
    spread = lax.psum_scatter(diag_term + placed, ("grid", "pole"), scatter_dimension=0, tiled=True)
    diag_share = lax.all_gather(spread, "pole", axis=0, tiled=True)
    return (panel_share, diag_share)


def fused_kernel(
    grid_size, pole_size, ancestors, weight, pool, tiles, diag_in,
    panel_out, diag_out,
    rows, sent_panel, got_panel, column, own_diag, sent_diag, diag_local, pole_sums, grid_send, grid_sums, final,
    pool_sem, tile_sem, diag_sem, up_sem, down_sem, arrive_sem,
    panel_send, panel_recv, a_send, a_recv, b_send, b_recv, c_send, c_recv, *factors,
):
    g = lax.axis_index("grid")
    q = lax.axis_index("pole")
    supers, listed_count = ancestors.shape
    half = factors[0].shape[3] // 2
    width = factors[0].shape[2]
    slice_rows = width // grid_size
    share = width // pole_size
    blocks = rows.shape[2] // width
    chunks = [(k, c) for k in range(supers) for c in range(HALVES)]

    tile_copies = []
    for j, (k, c) in enumerate(chunks):
        for part in range(2):
            copy = pltpu.make_async_copy(
                tiles.at[0, k, part, :, :, pl.ds(c * half, half)],
                factors[k].at[c, :, pl.ds(g * slice_rows, slice_rows), pl.ds(part * half, half)],
                tile_sem.at[j, part],
            )
            copy.start()
            tile_copies.append(copy)
    pool_copies = []
    for part in range(2):
        for a in range(rows.shape[1]):
            copy = pltpu.make_async_copy(
                pool.at[0, part, :, pl.ds(a * width, width)], rows.at[part, a], pool_sem.at[part, a]
            )
            copy.start()
            pool_copies.append(copy)
    diag_copy = pltpu.make_async_copy(diag_in.at[0], diag_local, diag_sem)
    diag_copy.start()

    barrier = pltpu.get_barrier_semaphore()
    for step in range(1, grid_size):
        pl.semaphore_signal(
            barrier, inc=1, device_id={"grid": lax.rem(g + step, grid_size)}, device_id_type=MESH
        )
    for step in range(1, pole_size):
        pl.semaphore_signal(
            barrier, inc=1, device_id={"pole": lax.rem(q + step, pole_size)}, device_id_type=MESH
        )
    pl.semaphore_wait(barrier, grid_size - 1 + pole_size - 1)

    def piece(j, source):
        k, c = chunks[j]
        return factors[k].at[c, :, pl.ds(source * slice_rows, slice_rows), :]

    def hop(j, source, up):
        return pltpu.make_async_remote_copy(
            src_ref=piece(j, source),
            dst_ref=piece(j, source),
            send_sem=(up_sem if up else down_sem).at[j, source],
            recv_sem=arrive_sem.at[j, source],
            device_id={"grid": g + 1 if up else g - 1},
            device_id_type=MESH,
        )

    def pass_on(j, distance):
        low = g - distance
        high = g + distance
        if distance:
            @pl.when(low >= 0)
            def _():
                hop(j, low, True).wait_recv()

        @pl.when(jnp.logical_and(low >= 0, g + 1 < grid_size))
        def _():
            hop(j, low, True).start()

        if distance:
            @pl.when(high < grid_size)
            def _():
                hop(j, high, False).wait_recv()

        @pl.when(jnp.logical_and(high < grid_size, g >= 1))
        def _():
            hop(j, high, False).start()

    for j in range(len(chunks)):
        tile_copies[2 * j].wait()
        tile_copies[2 * j + 1].wait()
        pass_on(j, 0)
    for copy in pool_copies:
        copy.wait()
    diag_copy.wait()
    for distance in range(1, grid_size - 1):
        for j in range(len(chunks)):
            pass_on(j, distance)

    w_real = weight[0, 0]
    w_imag = weight[0, 1]

    def panel_copy(j, k, c, b):
        slot = lax.rem(q - k + pole_size, pole_size) - 1
        span = pl.ds(b * width, width)
        return pltpu.make_async_remote_copy(
            src_ref=sent_panel.at[k, c, span],
            dst_ref=got_panel.at[slot, c, span],
            send_sem=panel_send.at[j, b],
            recv_sem=panel_recv.at[slot, c, b],
            device_id={"pole": k},
            device_id_type=MESH,
        )

    def share_copy(k, r):
        return pltpu.make_async_remote_copy(
            src_ref=sent_diag.at[k, pl.ds(r * share, share)],
            dst_ref=pole_sums.at[k, q],
            send_sem=a_send.at[k, r],
            recv_sem=a_recv.at[k, q],
            device_id={"pole": r},
            device_id_type=MESH,
        )

    def place_of(k, block):
        count = jnp.int32(0)
        position = jnp.int32(0)
        for n in range(listed_count):
            hit = (ancestors[k, n] == block).astype(jnp.int32)
            count = count + hit
            position = position + hit * n
        return count, jnp.clip(position, 0, listed_count - 1)

    def grid_copy(k):
        return pltpu.make_async_remote_copy(
            src_ref=grid_send.at[k],
            dst_ref=grid_sums.at[g],
            send_sem=b_send.at[k],
            recv_sem=b_recv.at[g],
            device_id={"grid": k},
            device_id_type=MESH,
        )

    def final_copy(r):
        mine = pl.ds(pl.multiple_of(q * share, share), share)
        return pltpu.make_async_remote_copy(
            src_ref=final.at[mine],
            dst_ref=final.at[mine],
            send_sem=c_send.at[r],
            recv_sem=c_recv.at[q],
            device_id={"pole": r},
            device_id_type=MESH,
        )

    def landing(buffer, semaphore):
        return pltpu.make_async_remote_copy(
            src_ref=buffer, dst_ref=buffer, send_sem=semaphore, recv_sem=semaphore,
            device_id={"pole": q}, device_id_type=MESH,
        )

    def to_owner(k):
        for r in range(pole_size):
            @pl.when(q != r)
            def _():
                landing(pole_sums.at[k, r], a_recv.at[k, r]).wait_recv()
        summed = own_diag[k, pl.ds(pl.multiple_of(q * share, share), share), :]
        for step in range(1, pole_size):
            summed = summed + pole_sums[k, lax.rem(q + step, pole_size)].astype(jnp.float32)
        grid_send[k] = summed

        @pl.when(g != k)
        def _():
            grid_copy(k).start()

        @pl.when(g == k)
        def _():
            grid_sums[g] = grid_send[k]

    for j, (k, c) in enumerate(chunks):
        pass_on(j, grid_size - 1)

        @pl.loop(0, blocks)
        def _(b):
            span = pl.ds(pl.multiple_of(b * width, width), width)
            with_real = jnp.zeros((width, 2 * half), jnp.float32)
            with_imag = jnp.zeros((width, 2 * half), jnp.float32)
            for n in range(listed_count):
                source = jnp.clip(ancestors[k, n], 0, rows.shape[1] - 1)
                factor = factors[k][c, n]
                with_real += jnp.dot(
                    rows[0, source, span, :], factor, preferred_element_type=jnp.float32
                )
                with_imag += jnp.dot(
                    rows[1, source, span, :], factor, preferred_element_type=jnp.float32
                )
            count, _ = place_of(k, g * blocks + b)
            keep = jnp.full((width, half), count, jnp.int32) > 0
            real = jnp.where(keep, with_imag[:, half:] - with_real[:, :half], 0.0)
            imag = jnp.where(keep, -(with_real[:, half:] + with_imag[:, :half]), 0.0)
            column[span, pl.ds(c * 2 * half, half)] = real.astype(jnp.bfloat16)
            column[span, pl.ds(c * 2 * half + half, half)] = imag.astype(jnp.bfloat16)
            term = w_real * imag + w_imag * real
            sent_panel[k, c, span, :] = term.astype(jnp.bfloat16)

            @pl.when(q == k)
            def _():
                panel_out[span, pl.ds(c * half, half)] = term

            @pl.when(q != k)
            def _():
                panel_copy(j, k, c, b).start()

        if c == HALVES - 1:
            for left in range(HALVES):
                for right in range(HALVES):
                    def add(b, total):
                        _, position = place_of(k, g * blocks + b)
                        span = pl.ds(pl.multiple_of(b * width, width), width)
                        return total + lax.dot_general(
                            factors[k][left, position],
                            column[span, pl.ds(right * 2 * half, 2 * half)],
                            (((0,), (0,)), ((), ())),
                            preferred_element_type=jnp.float32,
                        )

                    total = jnp.zeros((2 * half, 2 * half), jnp.float32)
                    for b in range(blocks):
                        total = add(b, total)
                    real = total[half:, half:] - total[:half, :half]
                    imag = -(total[:half, half:] + total[half:, :half])
                    own_diag[k, pl.ds(left * half, half), pl.ds(right * half, half)] = (
                        w_real * imag + w_imag * real
                    )

            @pl.when(g == k)
            def _():
                own_diag[k] = (
                    own_diag[k]
                    + w_real * diag_local[1].astype(jnp.float32)
                    + w_imag * diag_local[0].astype(jnp.float32)
                )

            sent_diag[k] = own_diag[k].astype(jnp.bfloat16)
            for r in range(pole_size):
                @pl.when(q != r)
                def _():
                    share_copy(k, r).start()

            if k:
                to_owner(k - 1)

    to_owner(supers - 1)
    for s in range(grid_size):
        @pl.when(g != s)
        def _():
            landing(grid_sums.at[s], b_recv.at[s]).wait_recv()
    summed = grid_sums[0]
    for s in range(1, grid_size):
        summed = summed + grid_sums[s]
    final[pl.ds(pl.multiple_of(q * share, share), share), :] = summed
    for r in range(pole_size):
        @pl.when(q != r)
        def _():
            final_copy(r).start()

    for c in range(HALVES):
        @pl.loop(0, blocks)
        def _(b):
            span = pl.ds(pl.multiple_of(b * width, width), width)
            for slot in range(pole_size - 1):
                landing(got_panel.at[slot, c, span], panel_recv.at[slot, c, b]).wait_recv()
            lanes = pl.ds(c * half, half)
            total = panel_out[span, lanes]
            for slot in range(pole_size - 1):
                total = total + got_panel[slot, c, span, :].astype(jnp.float32)
            panel_out[span, lanes] = total

    for r in range(pole_size):
        @pl.when(q != r)
        def _():
            landing(final.at[pl.ds(r * share, share)], c_recv.at[r]).wait_recv()
    diag_out[...] = final[...]

    for distance in range(grid_size - 1):
        for j in range(len(chunks)):
            @pl.when(jnp.logical_and(g - distance >= 0, g + 1 < grid_size))
            def _():
                hop(j, g - distance, True).wait_send()

            @pl.when(jnp.logical_and(g + distance < grid_size, g >= 1))
            def _():
                hop(j, g + distance, False).wait_send()
    for j, (k, c) in enumerate(chunks):
        for b in range(blocks):
            @pl.when(q != k)
            def _():
                panel_copy(j, k, c, b).wait_send()
    for k in range(supers):
        for r in range(pole_size):
            @pl.when(q != r)
            def _():
                share_copy(k, r).wait_send()

        @pl.when(g != k)
        def _():
            grid_copy(k).wait_send()
    for r in range(pole_size):
        @pl.when(q != r)
        def _():
            final_copy(r).wait_send()


def fused(grid_size, pole_size, inverse_pool, factor_tiles, diag_inverse, pole_weight, ancestors):
    supers, listed_count = ancestors.shape
    width = factor_tiles.shape[5]
    height = inverse_pool.shape[2]
    half = width // HALVES
    share = width // pole_size
    chunks = supers * HALVES
    blocks = height // width
    dma = pltpu.SemaphoreType.DMA
    f32 = jnp.float32
    bf16 = jnp.bfloat16
    scratch = [
        pltpu.VMEM((2, inverse_pool.shape[3] // width, height, width), bf16),
        pltpu.VMEM((supers, HALVES, height, half), bf16),
        pltpu.VMEM((pole_size - 1, HALVES, height, half), bf16),
        pltpu.VMEM((height, 2 * width), bf16),
        pltpu.VMEM((supers, width, width), f32),
        pltpu.VMEM((supers, width, width), bf16),
        pltpu.VMEM(diag_inverse.shape[1:], bf16),
        pltpu.VMEM((supers, pole_size, share, width), bf16),
        pltpu.VMEM((supers, share, width), f32),
        pltpu.VMEM((grid_size, share, width), f32),
        pltpu.VMEM((width, width), f32),
        dma((2, inverse_pool.shape[3] // width)), dma((chunks, 2)), dma(()),
        dma((chunks, grid_size)), dma((chunks, grid_size)), dma((chunks, grid_size)),
        dma((chunks, blocks)), dma((pole_size - 1, HALVES, blocks)),
        dma((supers, pole_size)), dma((supers, pole_size)),
        dma((supers,)), dma((grid_size,)),
        dma((pole_size,)), dma((pole_size,)),
    ] + [pltpu.VMEM((HALVES, listed_count, width, 2 * half), bf16)] * supers
    smem = pl.BlockSpec(memory_space=pltpu.SMEM)
    vmem = pl.BlockSpec(memory_space=pltpu.VMEM)
    anywhere = pl.BlockSpec(memory_space=pl.ANY)
    return pl.pallas_call(
        functools.partial(fused_kernel, grid_size, pole_size),
        out_shape=(
            jax.ShapeDtypeStruct((height, width), f32),
            jax.ShapeDtypeStruct((width, width), f32),
        ),
        in_specs=[smem, smem, anywhere, anywhere, anywhere],
        out_specs=(vmem, vmem),
        scratch_shapes=scratch,
        compiler_params=pltpu.CompilerParams(
            collective_id=0, has_side_effects=True, vmem_limit_bytes=56 * 2**20
        ),
    )(ancestors, pole_weight, inverse_pool, factor_tiles, diag_inverse)


def choose(grid_size, pole_size, inverse_pool, factor_tiles, diag_inverse, pole_weight, ancestors):
    supers = ancestors.shape[0]
    width = factor_tiles.shape[5]
    whole_blocks = inverse_pool.shape[2] % width == 0 and factor_tiles.shape[4] % 16 == 0
    if whole_blocks and supers == grid_size == pole_size and width % (HALVES * 128) == 0:
        return fused(
            grid_size, pole_size, inverse_pool, factor_tiles, diag_inverse, pole_weight, ancestors
        )
    return shards(inverse_pool, factor_tiles, diag_inverse, pole_weight, ancestors)


def solution(mesh):
    in_specs = (
        P(("ens", "pole"), None, "grid", None),
        P(("ens", "pole"), None, None, None, "grid", None),
        P(("ens", "pole"), None, "grid", None),
        P("pole", None),
        P(),
    )
    out_specs = (P(("ens", "grid"), "pole"), P(("ens", "grid"), None))
    body = functools.partial(choose, mesh.shape["grid"], mesh.shape["pole"])
    return jax.shard_map(body, mesh=mesh, in_specs=in_specs, out_specs=out_specs, check_vma=False)
```

```python
import functools

import jax
import jax.numpy as jnp
from jax import lax
from jax.experimental import pallas as pl
from jax.experimental.pallas import tpu as pltpu
from jax.sharding import PartitionSpec as P

MESH = pl.DeviceIdType.MESH
HALVES = 2


def plain_product(left, right):
    return jnp.dot(left, right, preferred_element_type=jnp.float32)


def turned_product(left, right):
    return lax.dot_general(
        left, right, (((0,), (0,)), ((), ())), preferred_element_type=jnp.float32
    )


def portion_terms(rows_pair, block_index, offset, listed, factors, weights):
    tile_width = factors.shape[3]
    listed_count = factors.shape[1]
    height = rows_pair.shape[1]
    blocks = rows_pair.shape[2] // tile_width
    matches = listed == block_index

    def compute():
        chosen = rows_pair.reshape(2, height, blocks, tile_width)[:, :, listed, :].reshape(
            2, height, listed_count * tile_width
        )
        stacked = factors.reshape(2, listed_count * tile_width, tile_width)
        part_real = -(plain_product(chosen[0], stacked[0]) - plain_product(chosen[1], stacked[1]))
        part_imag = -(plain_product(chosen[0], stacked[1]) + plain_product(chosen[1], stacked[0]))
        panel_piece = weights[0] * part_imag + weights[1] * part_real
        rounded_real = part_real.astype(jnp.bfloat16)
        rounded_imag = part_imag.astype(jnp.bfloat16)
        position = jnp.sum(jnp.where(matches, jnp.arange(listed_count, dtype=jnp.int32), 0))
        matched = lax.dynamic_slice(
            factors, (jnp.int32(0), position, offset, jnp.int32(0)), (2, 1, height, tile_width)
        )[:, 0]
        diag_real = -(
            turned_product(matched[0], rounded_real) - turned_product(matched[1], rounded_imag)
        )
        diag_imag = -(
            turned_product(matched[0], rounded_imag) + turned_product(matched[1], rounded_real)
        )
        return (panel_piece, weights[0] * diag_imag + weights[1] * diag_real)

    def skipped():
        return (
            jnp.zeros((height, tile_width), jnp.float32),
            jnp.zeros((tile_width, tile_width), jnp.float32),
        )

    return lax.cond(jnp.any(matches), compute, skipped)


def rows_terms(rows_pair, row_first, listed, factors, weights):
    tile_width = factors.shape[3]
    height = rows_pair.shape[1]
    piece_rows = min(height, tile_width)
    panels = []
    diag_total = jnp.zeros((tile_width, tile_width), jnp.float32)
    for portion in range(height // piece_rows):
        row_start = row_first + portion * piece_rows
        panel_piece, diag_piece = portion_terms(
            rows_pair[:, portion * piece_rows : (portion + 1) * piece_rows],
            row_start // tile_width,
            row_start % tile_width,
            listed,
            factors,
            weights,
        )
        panels.append(panel_piece)
        diag_total = diag_total + diag_piece
    return (jnp.concatenate(panels, axis=0), diag_total)


def shards(inverse_pool, factor_tiles, diag_inverse, pole_weight, ancestors):
    device_index = lax.axis_index("grid")
    rows_here = inverse_pool.shape[2]
    supers = factor_tiles.shape[1]
    tile_width = factor_tiles.shape[5]
    row_slab = inverse_pool[0]
    weights = (pole_weight[0, 0], pole_weight[0, 1])
    row_first = device_index * rows_here
    own_panels = []
    diag_terms = []
    for supernode in range(supers):
        factors = lax.all_gather(factor_tiles[0, supernode], "grid", axis=2, tiled=True)
        listed = ancestors[supernode]
        own_panel, own_diag = rows_terms(row_slab, row_first, listed, factors, weights)
        diag_terms.append(own_diag)
        own_panels.append(own_panel)
    panel_rows = jnp.concatenate(own_panels, axis=1)
    panel_share = lax.psum_scatter(panel_rows, "pole", scatter_dimension=1, tiled=True)
    diag_term = jnp.stack(diag_terms, axis=0).reshape(supers * tile_width, tile_width)
    diag_local = diag_inverse[0]
    local_block = weights[0] * diag_local[1].astype(jnp.float32) + weights[1] * diag_local[
        0
    ].astype(jnp.float32)
    share_rows = local_block.shape[0]
    placed = lax.dynamic_update_slice(
        jnp.zeros_like(diag_term), local_block, (device_index * share_rows, jnp.int32(0))
    )
    spread = lax.psum_scatter(diag_term + placed, ("grid", "pole"), scatter_dimension=0, tiled=True)
    diag_share = lax.all_gather(spread, "pole", axis=0, tiled=True)
    return (panel_share, diag_share)


def fused_kernel(
    grid_size, pole_size, ancestors, weight, pool, tiles, diag_in,
    panel_out, diag_out,
    rows, sent_panel, got_panel, column, own_diag, sent_diag, diag_local, pole_sums, grid_send, grid_sums, final,
    pool_sem, tile_sem, diag_sem, up_sem, down_sem, arrive_sem,
    panel_send, panel_recv, a_send, a_recv, b_send, b_recv, c_send, c_recv, *factors,
):
    g = lax.axis_index("grid")
    q = lax.axis_index("pole")
    supers, listed_count = ancestors.shape
    half = factors[0].shape[3] // 2
    width = factors[0].shape[2]
    slice_rows = width // grid_size
    share = width // pole_size
    blocks = rows.shape[2] // width
    chunks = [(k, c) for k in range(supers) for c in range(HALVES)]

    tile_copies = []
    for j, (k, c) in enumerate(chunks):
        for part in range(2):
            copy = pltpu.make_async_copy(
                tiles.at[0, k, part, :, :, pl.ds(c * half, half)],
                factors[k].at[c, :, pl.ds(g * slice_rows, slice_rows), pl.ds(part * half, half)],
                tile_sem.at[j, part],
            )
            copy.start()
            tile_copies.append(copy)
    diag_copy = pltpu.make_async_copy(diag_in.at[0], diag_local, diag_sem)
    diag_copy.start()

    barrier = pltpu.get_barrier_semaphore()
    for step in range(1, grid_size):
        pl.semaphore_signal(
            barrier, inc=1, device_id={"grid": lax.rem(g + step, grid_size)}, device_id_type=MESH
        )
    for step in range(1, pole_size):
        pl.semaphore_signal(
            barrier, inc=1, device_id={"pole": lax.rem(q + step, pole_size)}, device_id_type=MESH
        )
    pl.semaphore_wait(barrier, grid_size - 1 + pole_size - 1)

    def piece(j, source):
        k, c = chunks[j]
        return factors[k].at[c, :, pl.ds(source * slice_rows, slice_rows), :]

    def hop(j, source, up):
        return pltpu.make_async_remote_copy(
            src_ref=piece(j, source),
            dst_ref=piece(j, source),
            send_sem=(up_sem if up else down_sem).at[j, source],
            recv_sem=arrive_sem.at[j, source],
            device_id={"grid": g + 1 if up else g - 1},
            device_id_type=MESH,
        )

    def pass_on(j, distance):
        low = g - distance
        high = g + distance
        if distance:
            @pl.when(low >= 0)
            def _():
                hop(j, low, True).wait_recv()

        @pl.when(jnp.logical_and(low >= 0, g + 1 < grid_size))
        def _():
            hop(j, low, True).start()

        if distance:
            @pl.when(high < grid_size)
            def _():
                hop(j, high, False).wait_recv()

        @pl.when(jnp.logical_and(high < grid_size, g >= 1))
        def _():
            hop(j, high, False).start()

    for j in range(len(chunks)):
        tile_copies[2 * j].wait()
        tile_copies[2 * j + 1].wait()
        pass_on(j, 0)
    pool_copies = []
    for part in range(2):
        for a in range(rows.shape[1]):
            copy = pltpu.make_async_copy(
                pool.at[0, part, :, pl.ds(a * width, width)], rows.at[part, a], pool_sem.at[part, a]
            )
            copy.start()
            pool_copies.append(copy)
    for distance in range(1, grid_size - 1):
        for j in range(len(chunks)):
            pass_on(j, distance)
    for copy in pool_copies:
        copy.wait()
    diag_copy.wait()

    w_real = weight[0, 0]
    w_imag = weight[0, 1]

    def panel_copy(j, k, c, b):
        slot = lax.rem(q - k + pole_size, pole_size) - 1
        span = pl.ds(b * width, width)
        return pltpu.make_async_remote_copy(
            src_ref=sent_panel.at[k, c, span],
            dst_ref=got_panel.at[slot, c, span],
            send_sem=panel_send.at[j, b],
            recv_sem=panel_recv.at[slot, c, b],
            device_id={"pole": k},
            device_id_type=MESH,
        )

    def share_copy(k, r):
        return pltpu.make_async_remote_copy(
            src_ref=sent_diag.at[k, pl.ds(r * share, share)],
            dst_ref=pole_sums.at[k, q],
            send_sem=a_send.at[k, r],
            recv_sem=a_recv.at[k, q],
            device_id={"pole": r},
            device_id_type=MESH,
        )

    def place_of(k, block):
        count = jnp.int32(0)
        position = jnp.int32(0)
        for n in range(listed_count):
            hit = (ancestors[k, n] == block).astype(jnp.int32)
            count = count + hit
            position = position + hit * n
        return count, jnp.clip(position, 0, listed_count - 1)

    def grid_copy(k):
        return pltpu.make_async_remote_copy(
            src_ref=grid_send.at[k],
            dst_ref=grid_sums.at[g],
            send_sem=b_send.at[k],
            recv_sem=b_recv.at[g],
            device_id={"grid": k},
            device_id_type=MESH,
        )

    def final_copy(r):
        mine = pl.ds(pl.multiple_of(q * share, share), share)
        return pltpu.make_async_remote_copy(
            src_ref=final.at[mine],
            dst_ref=final.at[mine],
            send_sem=c_send.at[r],
            recv_sem=c_recv.at[q],
            device_id={"pole": r},
            device_id_type=MESH,
        )

    def landing(buffer, semaphore):
        return pltpu.make_async_remote_copy(
            src_ref=buffer, dst_ref=buffer, send_sem=semaphore, recv_sem=semaphore,
            device_id={"pole": q}, device_id_type=MESH,
        )

    def to_owner(k):
        for r in range(pole_size):
            @pl.when(q != r)
            def _():
                landing(pole_sums.at[k, r], a_recv.at[k, r]).wait_recv()
        summed = own_diag[k, pl.ds(pl.multiple_of(q * share, share), share), :]
        for step in range(1, pole_size):
            summed = summed + pole_sums[k, lax.rem(q + step, pole_size)].astype(jnp.float32)
        grid_send[k] = summed

        @pl.when(g != k)
        def _():
            grid_copy(k).start()

        @pl.when(g == k)
        def _():
            grid_sums[g] = grid_send[k]

    for j, (k, c) in enumerate(chunks):
        pass_on(j, grid_size - 1)

        @pl.loop(0, blocks)
        def _(b):
            span = pl.ds(pl.multiple_of(b * width, width), width)
            with_real = jnp.zeros((width, 2 * half), jnp.float32)
            with_imag = jnp.zeros((width, 2 * half), jnp.float32)
            for n in range(listed_count):
                source = jnp.clip(ancestors[k, n], 0, rows.shape[1] - 1)
                factor = factors[k][c, n]
                with_real += jnp.dot(
                    rows[0, source, span, :], factor, preferred_element_type=jnp.float32
                )
                with_imag += jnp.dot(
                    rows[1, source, span, :], factor, preferred_element_type=jnp.float32
                )
            count, _ = place_of(k, g * blocks + b)
            keep = jnp.full((width, half), count, jnp.int32) > 0
            real = jnp.where(keep, with_imag[:, half:] - with_real[:, :half], 0.0)
            imag = jnp.where(keep, -(with_real[:, half:] + with_imag[:, :half]), 0.0)
            column[span, pl.ds(c * 2 * half, half)] = real.astype(jnp.bfloat16)
            column[span, pl.ds(c * 2 * half + half, half)] = imag.astype(jnp.bfloat16)
            term = w_real * imag + w_imag * real
            sent_panel[k, c, span, :] = term.astype(jnp.bfloat16)

            @pl.when(q == k)
            def _():
                panel_out[span, pl.ds(c * half, half)] = term

            @pl.when(q != k)
            def _():
                panel_copy(j, k, c, b).start()

        if c == HALVES - 1:
            for left in range(HALVES):
                for right in range(HALVES):
                    def add(b, total):
                        _, position = place_of(k, g * blocks + b)
                        span = pl.ds(pl.multiple_of(b * width, width), width)
                        return total + lax.dot_general(
                            factors[k][left, position],
                            column[span, pl.ds(right * 2 * half, 2 * half)],
                            (((0,), (0,)), ((), ())),
                            preferred_element_type=jnp.float32,
                        )

                    total = jnp.zeros((2 * half, 2 * half), jnp.float32)
                    for b in range(blocks):
                        total = add(b, total)
                    real = total[half:, half:] - total[:half, :half]
                    imag = -(total[:half, half:] + total[half:, :half])
                    own_diag[k, pl.ds(left * half, half), pl.ds(right * half, half)] = (
                        w_real * imag + w_imag * real
                    )

            @pl.when(g == k)
            def _():
                own_diag[k] = (
                    own_diag[k]
                    + w_real * diag_local[1].astype(jnp.float32)
                    + w_imag * diag_local[0].astype(jnp.float32)
                )

            sent_diag[k] = own_diag[k].astype(jnp.bfloat16)
            for r in range(pole_size):
                @pl.when(q != r)
                def _():
                    share_copy(k, r).start()

            if k:
                to_owner(k - 1)

    to_owner(supers - 1)
    for s in range(grid_size):
        @pl.when(g != s)
        def _():
            landing(grid_sums.at[s], b_recv.at[s]).wait_recv()
    summed = grid_sums[0]
    for s in range(1, grid_size):
        summed = summed + grid_sums[s]
    final[pl.ds(pl.multiple_of(q * share, share), share), :] = summed
    for r in range(pole_size):
        @pl.when(q != r)
        def _():
            final_copy(r).start()

    for c in range(HALVES):
        @pl.loop(0, blocks)
        def _(b):
            span = pl.ds(pl.multiple_of(b * width, width), width)
            for slot in range(pole_size - 1):
                landing(got_panel.at[slot, c, span], panel_recv.at[slot, c, b]).wait_recv()
            lanes = pl.ds(c * half, half)
            total = panel_out[span, lanes]
            for slot in range(pole_size - 1):
                total = total + got_panel[slot, c, span, :].astype(jnp.float32)
            panel_out[span, lanes] = total

    for r in range(pole_size):
        @pl.when(q != r)
        def _():
            landing(final.at[pl.ds(r * share, share)], c_recv.at[r]).wait_recv()
    diag_out[...] = final[...]

    for distance in range(grid_size - 1):
        for j in range(len(chunks)):
            @pl.when(jnp.logical_and(g - distance >= 0, g + 1 < grid_size))
            def _():
                hop(j, g - distance, True).wait_send()

            @pl.when(jnp.logical_and(g + distance < grid_size, g >= 1))
            def _():
                hop(j, g + distance, False).wait_send()
    for j, (k, c) in enumerate(chunks):
        for b in range(blocks):
            @pl.when(q != k)
            def _():
                panel_copy(j, k, c, b).wait_send()
    for k in range(supers):
        for r in range(pole_size):
            @pl.when(q != r)
            def _():
                share_copy(k, r).wait_send()

        @pl.when(g != k)
        def _():
            grid_copy(k).wait_send()
    for r in range(pole_size):
        @pl.when(q != r)
        def _():
            final_copy(r).wait_send()


def fused(grid_size, pole_size, inverse_pool, factor_tiles, diag_inverse, pole_weight, ancestors):
    supers, listed_count = ancestors.shape
    width = factor_tiles.shape[5]
    height = inverse_pool.shape[2]
    half = width // HALVES
    share = width // pole_size
    chunks = supers * HALVES
    blocks = height // width
    dma = pltpu.SemaphoreType.DMA
    f32 = jnp.float32
    bf16 = jnp.bfloat16
    scratch = [
        pltpu.VMEM((2, inverse_pool.shape[3] // width, height, width), bf16),
        pltpu.VMEM((supers, HALVES, height, half), bf16),
        pltpu.VMEM((pole_size - 1, HALVES, height, half), bf16),
        pltpu.VMEM((height, 2 * width), bf16),
        pltpu.VMEM((supers, width, width), f32),
        pltpu.VMEM((supers, width, width), bf16),
        pltpu.VMEM(diag_inverse.shape[1:], bf16),
        pltpu.VMEM((supers, pole_size, share, width), bf16),
        pltpu.VMEM((supers, share, width), f32),
        pltpu.VMEM((grid_size, share, width), f32),
        pltpu.VMEM((width, width), f32),
        dma((2, inverse_pool.shape[3] // width)), dma((chunks, 2)), dma(()),
        dma((chunks, grid_size)), dma((chunks, grid_size)), dma((chunks, grid_size)),
        dma((chunks, blocks)), dma((pole_size - 1, HALVES, blocks)),
        dma((supers, pole_size)), dma((supers, pole_size)),
        dma((supers,)), dma((grid_size,)),
        dma((pole_size,)), dma((pole_size,)),
    ] + [pltpu.VMEM((HALVES, listed_count, width, 2 * half), bf16)] * supers
    smem = pl.BlockSpec(memory_space=pltpu.SMEM)
    vmem = pl.BlockSpec(memory_space=pltpu.VMEM)
    anywhere = pl.BlockSpec(memory_space=pl.ANY)
    return pl.pallas_call(
        functools.partial(fused_kernel, grid_size, pole_size),
        out_shape=(
            jax.ShapeDtypeStruct((height, width), f32),
            jax.ShapeDtypeStruct((width, width), f32),
        ),
        in_specs=[smem, smem, anywhere, anywhere, anywhere],
        out_specs=(vmem, vmem),
        scratch_shapes=scratch,
        compiler_params=pltpu.CompilerParams(
            collective_id=0, has_side_effects=True, vmem_limit_bytes=56 * 2**20
        ),
    )(ancestors, pole_weight, inverse_pool, factor_tiles, diag_inverse)


def choose(grid_size, pole_size, inverse_pool, factor_tiles, diag_inverse, pole_weight, ancestors):
    supers = ancestors.shape[0]
    width = factor_tiles.shape[5]
    whole_blocks = inverse_pool.shape[2] % width == 0 and factor_tiles.shape[4] % 16 == 0
    if whole_blocks and supers == grid_size == pole_size and width % (HALVES * 128) == 0:
        return fused(
            grid_size, pole_size, inverse_pool, factor_tiles, diag_inverse, pole_weight, ancestors
        )
    return shards(inverse_pool, factor_tiles, diag_inverse, pole_weight, ancestors)


def solution(mesh):
    in_specs = (
        P(("ens", "pole"), None, "grid", None),
        P(("ens", "pole"), None, None, None, "grid", None),
        P(("ens", "pole"), None, "grid", None),
        P("pole", None),
        P(),
    )
    out_specs = (P(("ens", "grid"), "pole"), P(("ens", "grid"), None))
    body = functools.partial(choose, mesh.shape["grid"], mesh.shape["pole"])
    return jax.shard_map(body, mesh=mesh, in_specs=in_specs, out_specs=out_specs, check_vma=False)
```
